32 devices in a mesh: dp: 8 (over z, y), tensor: 4 (over x, core).
Axes of the slice: x: 2, y: 2, z: 4, core: 2. Of those that a mesh axis runs over, the one named last changes fastest.
Arguments:
- features: float32 [512, 49, 2048], P('dp', None, 'tensor'), may hold values from -6 to 6
- frame_clip: int32 [512], P('dp'), may hold values from -1 to 127, as said below
- reduce_first: float32 [2048, 512], P(None, 'tensor'), may hold values from -0.125 to 0.125
- gain_reduce: float32 [512], P('tensor'), may hold values from 0.5 to 1.5
- bias_reduce: float32 [512], P('tensor'), may hold values from -1.2 to 1.2
- motion_down: float32 [512, 32], P('tensor'), may hold values from -0.25 to 0.25
- motion_kernel: float32 [9, 32], replicated, may hold values from -3.5 to 3.5
- motion_up: float32 [32, 512], P(None, 'tensor'), may hold values from -3 to 3
- motion_bias: float32 [512], P('tensor'), may hold values from -4 to 4
- group_taps: float32 [4, 3, 128], P('tensor'), may hold values from -3 to 3
- group_spatial: float32 [4, 1152, 128], P('tensor'), may hold values from -0.1875 to 0.1875
- gain_groups: float32 [512], P('tensor'), may hold values from 0.5 to 1.5
- bias_groups: float32 [512], P('tensor'), may hold values from -1.2 to 1.2
- expand_first: float32 [512, 2048], P('tensor'), may hold values from -0.25 to 0.25
- gain_expand: float32 [2048], P('tensor'), may hold values from 0.5 to 1.5
- bias_expand: float32 [2048], P('tensor'), may hold values from -1.2 to 1.2
- reduce_second: float32 [2048, 512], P(None, 'tensor'), may hold values from -0.125 to 0.125
- gain_narrow: float32 [512], P('tensor'), may hold values from 0.5 to 1.5
- bias_narrow: float32 [512], P('tensor'), may hold values from -1.2 to 1.2
- spatial_second: float32 [4608, 512], P(None, 'tensor'), may hold values from -0.09375 to 0.09375
- gain_spatial: float32 [512], P('tensor'), may hold values from 0.5 to 1.5
- bias_spatial: float32 [512], P('tensor'), may hold values from -1.2 to 1.2
- expand_second: float32 [512, 2048], P('tensor'), may hold values from -0.25 to 0.25
- gain_output: float32 [2048], P('tensor'), may hold values from 0.5 to 1.5
- bias_output: float32 [2048], P('tensor'), may hold values from -1.2 to 1.2
- cotangent: float32 [512, 49, 2048], P('dp', None, 'tensor'), may hold values from -6 to 6
Outputs:
- output: float32 [512, 49, 2048], P('dp', None, 'tensor')
- grad_features: float32 [512, 49, 2048], P('dp', None, 'tensor')
- grad_reduce_first: float32 [2048, 512], P(None, 'tensor')
- grad_gain_reduce: float32 [512], P('tensor')
- grad_bias_reduce: float32 [512], P('tensor')
- grad_motion_down: float32 [512, 32], P('tensor')
- grad_motion_kernel: float32 [9, 32], replicated
- grad_motion_up: float32 [32, 512], P(None, 'tensor')
- grad_motion_bias: float32 [512], P('tensor')
- grad_group_taps: float32 [4, 3, 128], P('tensor')
- grad_group_spatial: float32 [4, 1152, 128], P('tensor')
- grad_gain_groups: float32 [512], P('tensor')
- grad_bias_groups: float32 [512], P('tensor')
- grad_expand_first: float32 [512, 2048], P('tensor')
- grad_gain_expand: float32 [2048], P('tensor')
- grad_bias_expand: float32 [2048], P('tensor')
- grad_reduce_second: float32 [2048, 512], P(None, 'tensor')
- grad_gain_narrow: float32 [512], P('tensor')
- grad_bias_narrow: float32 [512], P('tensor')
- grad_spatial_second: float32 [4608, 512], P(None, 'tensor')
- grad_gain_spatial: float32 [512], P('tensor')
- grad_bias_spatial: float32 [512], P('tensor')
- grad_expand_second: float32 [512, 2048], P('tensor')
- grad_gain_output: float32 [2048], P('tensor')
- grad_bias_output: float32 [2048], P('tensor')
The draws below stay inside these ranges and needn't reach their ends.
Inputs may be any that keep to these rules, and one draw needn't show every extreme that they name: `frame_clip`: each device's 64 slots hold whole clips in consecutive slots, clip numbers differ between devices, every clip has 4 to 48 frames, every device's first clip has 48 frames, and -1 slots come after a device's last clip.
All inputs are finite; a program needn't handle non-finite values.
Results may differ from the reference program's by a relative error of at most 0.0095.
Values sent between devices are 32-bit elements; how exact they have to be, the bound alone decides.
A program may use at most 640 MiB of HBM per device.

```python
import jax
import jax.numpy as jnp
from jax import lax

C = 2048
M = 512
R = 32
GW = 128
SIDE = 7
MINLEN = 4
MAXLEN = 48
F_DEV = 64
GROUPS = 4
FRAMES = 512


def draw_frame_clip(key, part):
    devices = FRAMES // F_DEV
    most_clips = F_DEV // MINLEN
    key_len = jax.random.fold_in(key, 11)
    key_room = jax.random.fold_in(key, 23)
    lengths = jax.random.randint(key_len, (devices, most_clips), MINLEN, MAXLEN + 1)
    lengths = lengths.at[:, 0].set(MAXLEN)
    short_device = jax.random.randint(key_room, (), 0, devices)
    room = F_DEV - (jnp.arange(devices, dtype=jnp.int32) == short_device).astype(jnp.int32)
    ends = jnp.cumsum(lengths, axis=1)
    slots = jnp.arange(F_DEV, dtype=jnp.int32)
    local_clip = jnp.sum((slots[None, :, None] >= ends[:, None, :]).astype(jnp.int32), axis=2)
    local_clip = jnp.minimum(local_clip, most_clips - 1)
    clip_end = jnp.take_along_axis(ends, local_clip, axis=1)
    device_ids = jnp.arange(devices, dtype=jnp.int32)[:, None]
    numbers = jnp.where(clip_end <= room[:, None], device_ids * most_clips + (most_clips - 1 - local_clip), -1)
    return numbers.reshape(-1).astype(jnp.int32)


def levels(key, shape, cuts, smallest, largest):
    def one(axis_at, shards_of):
        steps = jax.random.uniform(jax.random.fold_in(jax.random.fold_in(key, 6), axis_at), (shards_of,), jnp.float32, smallest / len(cuts), largest / len(cuts))
        return jnp.repeat(jnp.exp(steps), shape[axis_at] // shards_of).reshape((-1,) + (1,) * (len(shape) - axis_at - 1))

    level = one(*cuts[0])
    for cut in cuts[1:]:
        level = level * one(*cut)
    return level


def gaussian(rng, dims, spread, reach, shards=(), kind=jnp.bfloat16):
    entries = jax.random.normal(rng, dims, jnp.float32) * spread
    if len(shards) > 0:
        entries = levels(rng, dims, shards, -0.22, 0.18) * entries
    return jnp.clip(entries, min=-reach, max=reach).astype(kind)


def setup_inputs(seed: int = 0) -> dict:
    seeds = jax.random.split(jax.random.key(seed), 27)
    features = gaussian(seeds[0], (FRAMES, SIDE * SIDE, C), 1.0, 6.0, ((0, 8), (2, 4)), jnp.float32)
    frame_clip = draw_frame_clip(jax.random.fold_in(seeds[26], 71), 0)
    reduce_first = gaussian(seeds[2], (C, M), C ** -0.5, 0.125, ((1, 4),), jnp.float32)
    gain_reduce = jnp.clip(1.0 + 0.1 * jax.random.normal(seeds[3], (M,), jnp.float32), 0.5, 1.5)
    bias_reduce = gaussian(seeds[4], (M,), 0.3, 1.2, ((0, 4),), jnp.float32)
    motion_down = gaussian(seeds[5], (M, R), M ** -0.5, 0.25, ((0, 4),), jnp.float32)
    motion_kernel = gaussian(seeds[6], (9, R), 3 ** -0.5, 3.5, (), jnp.float32)
    motion_up = gaussian(seeds[7], (R, M), (max(R // 8, 1)) ** -0.5, 3.0, ((1, 4),), jnp.float32)
    motion_bias = gaussian(seeds[8], (M,), 1.0, 4.0, ((0, 4),), jnp.float32)
    group_taps = gaussian(seeds[9], (GROUPS, 3, GW), 0.6, 3.0, ((0, 4),), jnp.float32)
    group_spatial = gaussian(seeds[10], (GROUPS, 9 * GW, GW), (9 * GW) ** -0.5, 0.1875, ((0, 4),), jnp.float32)
    gain_groups = jnp.clip(1.0 + 0.1 * jax.random.normal(seeds[11], (M,), jnp.float32), 0.5, 1.5)
    bias_groups = gaussian(seeds[12], (M,), 0.3, 1.2, ((0, 4),), jnp.float32)
    expand_first = gaussian(seeds[13], (M, C), M ** -0.5, 0.25, ((0, 4),), jnp.float32)
    gain_expand = jnp.clip(1.0 + 0.1 * jax.random.normal(seeds[14], (C,), jnp.float32), 0.5, 1.5)
    bias_expand = gaussian(seeds[15], (C,), 0.3, 1.2, ((0, 4),), jnp.float32)
    reduce_second = gaussian(seeds[16], (C, M), C ** -0.5, 0.125, ((1, 4),), jnp.float32)
    gain_narrow = jnp.clip(1.0 + 0.1 * jax.random.normal(seeds[17], (M,), jnp.float32), 0.5, 1.5)
    bias_narrow = gaussian(seeds[18], (M,), 0.3, 1.2, ((0, 4),), jnp.float32)
    spatial_second = gaussian(seeds[19], (9 * M, M), (9 * M) ** -0.5, 0.09375, ((1, 4),), jnp.float32)
    gain_spatial = jnp.clip(1.0 + 0.1 * jax.random.normal(seeds[20], (M,), jnp.float32), 0.5, 1.5)
    bias_spatial = gaussian(seeds[21], (M,), 0.3, 1.2, ((0, 4),), jnp.float32)
    expand_second = gaussian(seeds[22], (M, C), M ** -0.5, 0.25, ((0, 4),), jnp.float32)
    gain_output = jnp.clip(1.0 + 0.1 * jax.random.normal(seeds[23], (C,), jnp.float32), 0.5, 1.5)
    bias_output = gaussian(seeds[24], (C,), 0.3, 1.2, ((0, 4),), jnp.float32)
    cotangent = gaussian(seeds[25], (FRAMES, SIDE * SIDE, C), 1.0, 6.0, ((0, 8), (2, 4)), jnp.float32)
    return dict(features=features, frame_clip=frame_clip, reduce_first=reduce_first, gain_reduce=gain_reduce, bias_reduce=bias_reduce, motion_down=motion_down, motion_kernel=motion_kernel, motion_up=motion_up, motion_bias=motion_bias, group_taps=group_taps, group_spatial=group_spatial, gain_groups=gain_groups, bias_groups=bias_groups, expand_first=expand_first, gain_expand=gain_expand, bias_expand=bias_expand, reduce_second=reduce_second, gain_narrow=gain_narrow, bias_narrow=bias_narrow, spatial_second=spatial_second, gain_spatial=gain_spatial, bias_spatial=bias_spatial, expand_second=expand_second, gain_output=gain_output, bias_output=bias_output, cotangent=cotangent)


HIGH = lax.Precision.HIGHEST
EPS = 1e-05

def dense(values, weight):
    flat = values.reshape(-1, values.shape[-1])
    return jnp.dot(flat, weight, precision=HIGH).reshape(values.shape[:-1] + (weight.shape[1],))

def frame_taps(values):
    frames, cells, chans = values.shape
    grid = values.reshape(frames, SIDE, SIDE, chans)
    padded = jnp.pad(grid, ((0, 0), (1, 1), (1, 1), (0, 0)))
    return [padded[:, row:row + SIDE, col:col + SIDE, :].reshape(frames, cells, chans) for row in range(3) for col in range(3)]

def stack_taps(values):
    return jnp.concatenate(frame_taps(values), axis=-1)

def depthwise(values, kernel):
    pieces = frame_taps(values)
    total = pieces[0] * kernel[0]
    for index in range(1, 9):
        total = total + pieces[index] * kernel[index]
    return total

def next_frame(values):
    return jnp.concatenate([values[1:], jnp.zeros_like(values[:1])], axis=0)

def prev_frame(values):
    return jnp.concatenate([jnp.zeros_like(values[:1]), values[:-1]], axis=0)

def temporal(values, kernel, prev_same, next_same):
    return kernel[0] * prev_frame(values) * prev_same + kernel[1] * values + kernel[2] * next_frame(values) * next_same

def group_conv(values, kernel, weight, prev_same, next_same):
    return dense(stack_taps(temporal(values, kernel, prev_same, next_same)), weight)

def batch_norm(values, mrow, count, gain, bias):
    mean = lax.optimization_barrier(jnp.sum(values * mrow, axis=(0, 1))) / count
    centered = values - mean
    var = lax.optimization_barrier(jnp.sum(mrow * centered * centered, axis=(0, 1))) / count
    return gain * centered * lax.rsqrt(var + EPS) + bias

def reference(features, frame_clip, reduce_first, gain_reduce, bias_reduce, motion_down, motion_kernel, motion_up, motion_bias, group_taps, group_spatial, gain_groups, bias_groups, expand_first, gain_expand, bias_expand, reduce_second, gain_narrow, bias_narrow, spatial_second, gain_spatial, bias_spatial, expand_second, gain_output, bias_output, cotangent):
    valid = (frame_clip >= 0).astype(jnp.float32)
    after = jnp.concatenate([frame_clip[1:], jnp.full((1,), -2, jnp.int32)])
    before = jnp.concatenate([jnp.full((1,), -2, jnp.int32), frame_clip[:-1]])
    next_same = ((frame_clip >= 0) & (after == frame_clip)).astype(jnp.float32)[:, None, None]
    prev_same = ((frame_clip >= 0) & (before == frame_clip)).astype(jnp.float32)[:, None, None]
    mrow = valid[:, None, None]
    count = jnp.sum(valid) * (SIDE * SIDE)

    def forward(features, reduce_first, gain_reduce, bias_reduce, motion_down, motion_kernel, motion_up, motion_bias, group_taps, group_spatial, gain_groups, bias_groups, expand_first, gain_expand, bias_expand, reduce_second, gain_narrow, bias_narrow, spatial_second, gain_spatial, bias_spatial, expand_second, gain_output, bias_output):
        first_act = jax.nn.relu(batch_norm(dense(features, reduce_first), mrow, count, gain_reduce, bias_reduce))
        motion = dense(first_act, motion_down)
        shifted = next_frame(depthwise(motion, motion_kernel))
        pooled = lax.optimization_barrier(jnp.mean(next_same * (shifted - motion), axis=1))
        gate = jax.nn.sigmoid(jnp.dot(pooled, motion_up, precision=HIGH) + motion_bias)
        excited = first_act * gate[:, None, :]
        pieces = []
        carry = jnp.zeros(excited.shape[:-1] + (GW,), jnp.float32)
        for group in range(GROUPS):
            inputs = excited[:, :, group * GW:(group + 1) * GW] + carry
            carry = group_conv(inputs, group_taps[group], group_spatial[group], prev_same, next_same)
            pieces.append(carry)
        grouped = jnp.concatenate(pieces, axis=-1)
        mixed = jax.nn.relu(batch_norm(grouped, mrow, count, gain_groups, bias_groups))
        middle = jax.nn.relu(batch_norm(dense(mixed, expand_first), mrow, count, gain_expand, bias_expand) + features)
        narrow = jax.nn.relu(batch_norm(dense(middle, reduce_second), mrow, count, gain_narrow, bias_narrow))
        conv_act = jax.nn.relu(batch_norm(dense(stack_taps(narrow), spatial_second), mrow, count, gain_spatial, bias_spatial))
        final = batch_norm(dense(conv_act, expand_second), mrow, count, gain_output, bias_output)
        return mrow * jax.nn.relu(final + middle)
    output, pull = jax.vjp(forward, features, reduce_first, gain_reduce, bias_reduce, motion_down, motion_kernel, motion_up, motion_bias, group_taps, group_spatial, gain_groups, bias_groups, expand_first, gain_expand, bias_expand, reduce_second, gain_narrow, bias_narrow, spatial_second, gain_spatial, bias_spatial, expand_second, gain_output, bias_output)
    grads = pull(cotangent)
    return (output, grads[0], grads[1], grads[2], grads[3], grads[4], grads[5], grads[6], grads[7], grads[8], grads[9], grads[10], grads[11], grads[12], grads[13], grads[14], grads[15], grads[16], grads[17], grads[18], grads[19], grads[20], grads[21], grads[22], grads[23])
```

```python
import jax
import jax.numpy as jnp
import numpy as np
from jax import lax
from jax.sharding import PartitionSpec as P

SIDE = 7
CELLS = SIDE * SIDE
EPS = 1e-05
FWD = lax.Precision.HIGHEST
BWD = lax.Precision.HIGH
GRAD = lax.Precision.DEFAULT
BOTH = ("dp", "tensor")


def edge_mask():
    mask = np.zeros((CELLS, 9), np.float32)
    for row in range(SIDE):
        for col in range(SIDE):
            for a in range(3):
                for b in range(3):
                    if 0 <= row - (a - 1) < SIDE and 0 <= col - (b - 1) < SIDE:
                        mask[row * SIDE + col, a * 3 + b] = 1.0
    return mask


def mm(values, weight, precision):
    return lax.dot_general(values, weight, (((values.ndim - 1,), (0,)), ((), ())), precision=precision)


def mm_t(values, weight, precision):
    return lax.dot_general(values, weight, (((values.ndim - 1,), (1,)), ((), ())), precision=precision)


def outer(left, right, precision):
    return lax.dot_general(left, right, (((0, 1), (0, 1)), ((), ())), precision=precision)


def stack9(x):
    cells, frames, chans = x.shape
    grid = jnp.pad(x.reshape(SIDE, SIDE, frames, chans), ((1, 1), (1, 1), (0, 0), (0, 0)))
    return jnp.concatenate(
        [
            grid[row : row + SIDE, col : col + SIDE].reshape(cells, frames, chans)
            for row in range(3)
            for col in range(3)
        ],
        axis=-1,
    )


def flip_taps(weight, chans):
    outs = weight.shape[1]
    return weight.reshape(9, chans, outs)[::-1].transpose(0, 2, 1).reshape(9 * outs, chans)


def moments(h, mask, count, axes):
    local = jnp.sum(mask) * CELLS
    total = jnp.sum(h * mask, axis=(0, 1))
    mean = total / jnp.maximum(local, 1.0)
    second = jnp.sum(mask * (h - mean) ** 2, axis=(0, 1))
    local_row = jnp.full_like(mean, local)
    all_parts = lax.all_gather(jnp.stack([mean, second, local_row]), axes)
    means, seconds, counts = all_parts[:, 0], all_parts[:, 1], all_parts[:, 2]
    mean = jnp.sum(means * counts, axis=0) / count
    var = (jnp.sum(seconds, axis=0) + jnp.sum(counts * (means - mean) ** 2, axis=0)) / count
    return mean, lax.rsqrt(var + EPS)


def norm_back(grad, xhat, mask, gain, rstd, count, axes):
    sums = jnp.stack([jnp.sum(grad, axis=(0, 1)), jnp.sum(grad * xhat, axis=(0, 1))])
    sums = lax.psum(sums, axes)
    back = gain * rstd * (grad - mask * (sums[0] + xhat * sums[1]) / count)
    return back, sums[1], sums[0]


def reduce_frames(partial):
    return lax.psum_scatter(partial, "tensor", scatter_dimension=1, tiled=True)


def gather_frames(part):
    return lax.all_gather(part, "tensor", axis=1, tiled=True)


def shift_from(value, steps):
    count = lax.axis_size("tensor")
    initial, last = (max(0, -steps), min(count, count - steps))
    return lax.ppermute(value, "tensor", [(s, s + steps) for s in range(initial, last)])


def halo(x, width):
    left = shift_from(x[:, x.shape[1] - width :], 1)
    right = shift_from(x[:, :width], -1)
    return jnp.concatenate([left, x, right], axis=1)


def later(x):
    return jnp.concatenate([x[:, 1:], jnp.zeros_like(x[:, :1])], axis=1)


def earlier(x):
    return jnp.concatenate([jnp.zeros_like(x[:, :1]), x[:, :-1]], axis=1)


def local(
    features, frame_clip, reduce_first, gain_reduce, bias_reduce, motion_down, motion_kernel, motion_up,
    motion_bias, group_taps, group_spatial, gain_groups, bias_groups, expand_first, gain_expand, bias_expand,
    reduce_second, gain_narrow, bias_narrow, spatial_second, gain_spatial, bias_spatial, expand_second,
    gain_output, bias_output, cotangent,
):
    tensor = lax.axis_size("tensor")
    at = lax.axis_index("tensor")
    frames = features.shape[0]
    own = frames // tensor
    gw = group_taps.shape[2]
    rank = motion_down.shape[1]
    groups = tensor
    reach = groups
    x = jnp.transpose(features, (1, 0, 2))
    seed = jnp.transpose(cotangent, (1, 0, 2))

    valid = (frame_clip >= 0).astype(jnp.float32)
    count = lax.psum(jnp.sum(valid) * CELLS, "dp")
    wide_mask = valid[None, :, None]
    padded = jnp.pad(frame_clip, (reach + 1, reach + 1), constant_values=-2)
    clips = lax.dynamic_slice(padded, (at * own,), (own + 2 * reach + 2,))
    here = clips[1:-1]
    next_ext = ((here >= 0) & (clips[2:] == here)).astype(jnp.float32)[None, :, None]
    prev_ext = ((here >= 0) & (clips[:-2] == here)).astype(jnp.float32)[None, :, None]
    mask = (here >= 0).astype(jnp.float32)[reach : reach + own][None, :, None]
    next_own = next_ext[0, reach : reach + own]

    rows = lambda w: lax.all_to_all(w, "tensor", 0, 1, tiled=True)
    cols = lambda w: lax.all_to_all(w, "tensor", 1, 0, tiled=True)
    w_reduce, w_reduce2 = rows(reduce_first), rows(reduce_second)
    w_expand, w_expand2 = cols(expand_first), cols(expand_second)
    small = jnp.concatenate(
        [
            motion_down.T, motion_up, motion_bias[None], gain_reduce[None], bias_reduce[None], gain_groups[None],
            bias_groups[None], gain_narrow[None], bias_narrow[None], gain_spatial[None], bias_spatial[None],
            group_taps[0],
        ],
        axis=0,
    )
    small = lax.all_gather(small, "tensor", axis=1, tiled=True)
    md, mu = small[:rank].T, small[rank : 2 * rank]
    mb, g_red, b_red, g_grp, b_grp, g_nar, b_nar, g_spa, b_spa = [small[2 * rank + i] for i in range(9)]
    taps = small[2 * rank + 9 : 2 * rank + 12]
    spatial = lax.all_gather(spatial_second, "tensor", axis=1, tiled=True)
    group_w = lax.all_gather(group_spatial, "tensor", axis=0, tiled=True)

    h1 = reduce_frames(mm(x, w_reduce, FWD))
    mean1, r1 = moments(h1, mask, count, BOTH)
    xh1 = (h1 - mean1) * r1
    n1 = g_red * xh1 + b_red
    act1 = jnp.maximum(n1, 0.0)

    edges = jnp.asarray(edge_mask())
    w_pos = jnp.sum(edges[:, :, None] * motion_kernel[None], axis=1)
    motion = mm(act1, md, FWD)
    ahead = jnp.sum(motion * w_pos[:, None, :], axis=0)
    base = jnp.sum(motion, axis=0)
    follow = jnp.concatenate([ahead[1:], shift_from(ahead[:1], -1)], axis=0)
    pooled = next_own * (follow - base) / CELLS
    gate = jax.nn.sigmoid(jnp.dot(pooled, mu, precision=FWD) + mb)
    excited = act1 * gate[None]
    exc = halo(excited, reach)
    ins, mids, outs = [], [], []
    carry = 0.0
    mine = slice(reach, reach + own)
    for g in range(groups):
        part = slice(g * gw, (g + 1) * gw)
        u = exc[:, :, part] + carry
        k = taps[:, part]
        stacked = stack9(k[0] * earlier(u) * prev_ext + k[1] * u + k[2] * later(u) * next_ext)
        carry = mm(stacked, group_w[g], FWD)
        ins.append(u)
        mids.append(stacked[:, mine])
        outs.append(carry[:, mine])
    grouped = jnp.concatenate(outs, axis=-1)
    mean2, r2 = moments(grouped, mask, count, BOTH)
    xh2 = (grouped - mean2) * r2
    n2 = g_grp * xh2 + b_grp
    mixed = gather_frames(jnp.maximum(n2, 0.0))
    h3 = mm(mixed, w_expand, FWD)
    mean3, r3 = moments(h3, wide_mask, count, "dp")
    xh3 = (h3 - mean3) * r3
    pre3 = gain_expand * xh3 + bias_expand + x
    middle = jnp.maximum(pre3, 0.0)

    h4 = reduce_frames(mm(middle, w_reduce2, FWD))
    mean4, r4 = moments(h4, mask, count, BOTH)
    xh4 = (h4 - mean4) * r4
    n4 = g_nar * xh4 + b_nar
    stacked4 = stack9(jnp.maximum(n4, 0.0))
    h5 = mm(stacked4, spatial, FWD)
    mean5, r5 = moments(h5, mask, count, BOTH)
    xh5 = (h5 - mean5) * r5
    n5 = g_spa * xh5 + b_spa
    conv_act = gather_frames(jnp.maximum(n5, 0.0))
    h6 = mm(conv_act, w_expand2, FWD)
    mean6, r6 = moments(h6, wide_mask, count, "dp")
    xh6 = (h6 - mean6) * r6
    pre6 = gain_output * xh6 + bias_output + middle
    output = wide_mask * jnp.maximum(pre6, 0.0)

    d_last = jnp.where(pre6 > 0, seed * wide_mask, 0.0)
    d6, gg_output, gb_output = norm_back(d_last, xh6, wide_mask, gain_output, r6, count, "dp")
    gw_expand2 = outer(conv_act, d6, GRAD)
    d_n5 = jnp.where(n5 > 0, reduce_frames(mm_t(d6, w_expand2, BWD)), 0.0)
    d5, gg_spa, gb_spa = norm_back(d_n5, xh5, mask, g_spa, r5, count, BOTH)
    gw_spatial = outer(stacked4, d5, GRAD)
    d_n4 = jnp.where(n4 > 0, mm(stack9(d5), flip_taps(spatial, d5.shape[2]), BWD), 0.0)
    d4, gg_nar, gb_nar = norm_back(d_n4, xh4, mask, g_nar, r4, count, BOTH)
    d4_all = gather_frames(d4) * wide_mask
    gw_reduce2 = outer(middle, d4_all, GRAD)
    d_pre3 = jnp.where(pre3 > 0, d_last + mm_t(d4_all, w_reduce2, BWD), 0.0)

    d3, gg_expand, gb_expand = norm_back(d_pre3, xh3, wide_mask, gain_expand, r3, count, "dp")
    gw_expand = outer(mixed, d3, GRAD)
    d_n2 = jnp.where(n2 > 0, reduce_frames(mm_t(d3, w_expand, BWD)), 0.0)
    d2, gg_grp, gb_grp = norm_back(d_n2, xh2, mask, g_grp, r2, count, BOTH)
    d2_ext = halo(d2, reach)
    d_exc, gw_group, g_taps = [None] * groups, [None] * groups, [None] * groups
    carry = 0.0
    for g in reversed(range(groups)):
        part = slice(g * gw, (g + 1) * gw)
        k = taps[:, part]
        dy = d2_ext[:, :, part] + carry
        gw_group[g] = outer(mids[g], dy[:, mine], GRAD)
        dt = mm(stack9(dy), flip_taps(group_w[g], gw), BWD)
        u = ins[g]
        g_taps[g] = jnp.stack(
            [
                jnp.sum((dt * prev_ext * earlier(u))[:, mine], axis=(0, 1)),
                jnp.sum((dt * u)[:, mine], axis=(0, 1)),
                jnp.sum((dt * next_ext * later(u))[:, mine], axis=(0, 1)),
            ]
        )
        carry = k[0] * later(dt * prev_ext) + k[1] * dt + k[2] * earlier(dt * next_ext)
        d_exc[g] = carry[:, mine]
    d_exc = jnp.concatenate(d_exc, axis=-1)
    d_gate = jnp.sum(d_exc * act1, axis=0) * gate * (1.0 - gate)
    g_mb = jnp.sum(d_gate, axis=0)
    g_mu = lax.dot_general(pooled, d_gate, (((0,), (0,)), ((), ())), precision=FWD)
    d_pool = mm_t(d_gate, mu, FWD) * next_own / CELLS
    d_ahead = jnp.concatenate([shift_from(d_pool[-1:], 1), d_pool[:-1]], axis=0)
    g_pos = jnp.sum(motion * d_ahead[None], axis=1)
    g_mk = jnp.sum(edges[:, :, None] * g_pos[:, None, :], axis=0)
    d_motion = w_pos[:, None, :] * d_ahead[None] - d_pool[None]
    g_md = outer(act1, d_motion, FWD)
    d_n1 = jnp.where(n1 > 0, d_exc * gate[None] + mm_t(d_motion, md, FWD), 0.0)
    d1, gg_red, gb_red = norm_back(d_n1, xh1, mask, g_red, r1, count, BOTH)
    d1_all = gather_frames(d1) * wide_mask
    gw_reduce = outer(x, d1_all, GRAD)
    grad_features = d_pre3 + mm_t(d1_all, w_reduce, BWD)

    gw_spatial = lax.psum_scatter(gw_spatial, "tensor", scatter_dimension=1, tiled=True)
    gw_group = lax.psum_scatter(jnp.stack(gw_group), "tensor", scatter_dimension=0, tiled=True)
    big = lax.psum(
        (cols(gw_reduce), rows(gw_expand), cols(gw_reduce2), rows(gw_expand2), gw_spatial, gw_group), "dp"
    )
    tiny = jnp.concatenate([g_md.T, g_mu, g_mb[None], jnp.concatenate(g_taps, axis=-1)], axis=0)
    tiny, g_mk = lax.psum((tiny, g_mk), BOTH)
    narrow = jnp.stack([gg_red, gb_red, gg_grp, gb_grp, gg_nar, gb_nar, gg_spa, gb_spa])
    tiny = lax.dynamic_slice(jnp.concatenate([tiny, narrow]), (0, at * gw), (2 * rank + 12, gw))
    vec = tiny[2 * rank + 4 :]
    return (
        jnp.transpose(output, (1, 0, 2)),
        jnp.transpose(grad_features, (1, 0, 2)),
        big[0],
        vec[0],
        vec[1],
        tiny[:rank].T,
        g_mk,
        tiny[rank : 2 * rank],
        tiny[2 * rank],
        tiny[2 * rank + 1 : 2 * rank + 4][None],
        big[5],
        vec[2],
        vec[3],
        big[1],
        gg_expand,
        gb_expand,
        big[2],
        vec[4],
        vec[5],
        big[4],
        vec[6],
        vec[7],
        big[3],
        gg_output,
        gb_output,
    )


def solution(mesh):
    wide, col, row, chan, deep = P("dp", None, "tensor"), P(None, "tensor"), P("tensor", None), P("tensor"), P("tensor", None, None)
    return jax.shard_map(
        local,
        mesh=mesh,
        in_specs=(wide, P("dp"), col, chan, chan, row, P(), col, chan, deep, deep, chan, chan, row, chan, chan, col, chan, chan, col, chan, chan, row, chan, chan, wide),
        out_specs=(wide, wide, col, chan, chan, row, P(), col, chan, deep, deep, chan, chan, row, chan, chan, col, chan, chan, col, chan, chan, row, chan, chan),
        check_vma=False,
    )
```

```python
import functools

import jax
import jax.numpy as jnp
import numpy as np
from jax import lax
from jax.experimental import pallas as pl
from jax.experimental.pallas import tpu as pltpu
from jax.sharding import PartitionSpec as P

SIDE = 7
CELLS = SIDE * SIDE
EPS = 1e-05
FWD = lax.Precision.HIGHEST
BWD = lax.Precision.HIGH
GRAD = lax.Precision.DEFAULT
BOTH = ("dp", "tensor")


def edge_mask():
    mask = np.zeros((CELLS, 9), np.float32)
    for row in range(SIDE):
        for col in range(SIDE):
            for a in range(3):
                for b in range(3):
                    if 0 <= row - (a - 1) < SIDE and 0 <= col - (b - 1) < SIDE:
                        mask[row * SIDE + col, a * 3 + b] = 1.0
    return mask


def mm(values, weight, precision):
    return lax.dot_general(values, weight, (((values.ndim - 1,), (0,)), ((), ())), precision=precision)


def mm_t(values, weight, precision):
    return lax.dot_general(values, weight, (((values.ndim - 1,), (1,)), ((), ())), precision=precision)


def outer(left, right, precision):
    return lax.dot_general(left, right, (((0, 1), (0, 1)), ((), ())), precision=precision)


def stack9(x):
    cells, frames, chans = x.shape
    grid = jnp.pad(x.reshape(SIDE, SIDE, frames, chans), ((1, 1), (1, 1), (0, 0), (0, 0)))
    return jnp.concatenate(
        [
            grid[row : row + SIDE, col : col + SIDE].reshape(cells, frames, chans)
            for row in range(3)
            for col in range(3)
        ],
        axis=-1,
    )


def flip_taps(weight, chans):
    outs = weight.shape[1]
    return weight.reshape(9, chans, outs)[::-1].transpose(0, 2, 1).reshape(9 * outs, chans)


MESH = pl.DeviceIdType.MESH
ROWS = 7
CHUNKS = CELLS // ROWS
HBM = pl.BlockSpec(memory_space=pl.ANY)
VMEM = pl.BlockSpec(memory_space=pltpu.VMEM)
SMEM = pl.BlockSpec(memory_space=pltpu.SMEM)


def shape(*dims):
    return jax.ShapeDtypeStruct(dims, jnp.float32)


def params(number, megabytes):
    return pltpu.CompilerParams(collective_id=number, has_side_effects=True, vmem_limit_bytes=megabytes << 20)


class Group:
    def __init__(self, dp, tensor, whole):
        self.tensor = tensor
        self.whole = whole
        self.size = dp * tensor if whole else dp
        across, along = lax.axis_index("dp"), lax.axis_index("tensor")
        self.me = across * tensor + along if whole else across

    def device(self, flat):
        if self.whole:
            return {"dp": flat // self.tensor, "tensor": flat % self.tensor}
        return {"dp": flat}

    def others(self, act):
        def step(index, carry):
            act(self.device((self.me + index) % self.size))
            return carry

        lax.fori_loop(1, self.size, step, 0)

    def greet(self):
        barrier = pltpu.get_barrier_semaphore()
        self.others(lambda device: pl.semaphore_signal(barrier, 1, device_id=device, device_id_type=MESH))
        return barrier

    def meet(self, barrier):
        pl.semaphore_wait(barrier, self.size - 1)

    def exchange(self, note, box, sems):
        box[self.me] = note[...]
        self.others(
            lambda device: pltpu.make_async_remote_copy(
                src_ref=note, dst_ref=box.at[self.me], send_sem=sems.at[0], recv_sem=sems.at[1],
                device_id=device, device_id_type=MESH,
            ).start()
        )
        bulk = box.at[pl.ds(0, self.size - 1)]
        pltpu.make_async_copy(bulk, bulk, sems.at[1]).wait()
        pltpu.make_async_copy(bulk, bulk, sems.at[0]).wait()


def to_tile(note, first, second):
    for index in range(4):
        lanes = slice(index * 128, (index + 1) * 128)
        note[index : index + 1] = first[:, lanes]
        note[index + 4 : index + 5] = second[:, lanes]


def to_row(tile):
    return jnp.concatenate([tile[index : index + 1] for index in range(4)], axis=1)


def combine_moments(box, counts, size):
    total = counts[size]
    first = lax.fori_loop(0, size, lambda i, acc: acc + counts[i] * box[i], jnp.zeros((8, 128), jnp.float32))
    mean = first / total

    def step(i, acc):
        spread = box[i] - mean
        return acc[0] + box[i], acc[1] + counts[i] * spread * spread

    zero = jnp.zeros((8, 128), jnp.float32)
    inner, outer_part = lax.fori_loop(0, size, step, (zero, zero))
    var = (inner[4:8] + outer_part[0:4]) / total
    return mean[0:4], lax.rsqrt(var + EPS)


def positions(body, init):
    return lax.fori_loop(0, CELLS, body, init)


def scatter_frames(p, h, pair, cross, arrived, sems, along, own):
    mate, far = along + 1 - 2 * (along % 2), (along + 2) % 4
    far_mate = (mate + 2) % 4
    local, send_1, recv_1, send_2, recv_2 = sems

    def frames(device):
        return pl.ds(pl.multiple_of(device * own, own), own)

    def cut(k):
        return pl.ds(k * ROWS, ROWS)

    pairs = []
    for part, owner in ((0, far_mate), (1, mate)):
        row = []
        for k in range(CHUNKS):
            copy = pltpu.make_async_remote_copy(
                src_ref=p.at[cut(k), frames(owner)], dst_ref=pair.at[part, cut(k)], send_sem=send_1.at[part, k],
                recv_sem=recv_1.at[part, k], device_id={"tensor": mate}, device_id_type=MESH,
            )
            copy.start()
            row.append(copy)
        pairs.append(row)
    loads = []
    for part, (owner, target) in enumerate(((far, cross), (along, h))):
        copy = pltpu.make_async_copy(p.at[:, frames(owner)], target, local.at[part])
        copy.start()
        loads.append(copy)
    sends = [
        pltpu.make_async_remote_copy(
            src_ref=cross.at[cut(k)], dst_ref=arrived.at[cut(k)], send_sem=send_2.at[k], recv_sem=recv_2.at[k],
            device_id={"tensor": far}, device_id_type=MESH,
        )
        for k in range(CHUNKS)
    ]
    loads[0].wait()
    for k in range(CHUNKS):
        pairs[0][k].wait_recv()
        cross[cut(k)] = cross[cut(k)] + pair[0, cut(k)]
        if k:
            sends[k - 1].start()
    loads[1].wait()
    for k in range(CHUNKS):
        pairs[1][k].wait_recv()
        h[cut(k)] = h[cut(k)] + pair[1, cut(k)]
        if k == 0:
            sends[CHUNKS - 1].start()
    for k in range(CHUNKS):
        sends[k].wait_recv()
        h[cut(k)] = h[cut(k)] + arrived[cut(k)]
    for k in range(CHUNKS):
        sends[k].wait_send()
        pairs[0][k].wait_send()
        pairs[1][k].wait_send()


def gather_frames(fill, act, out, sems, along, own):
    mate, far = along + 1 - 2 * (along % 2), (along + 2) % 4
    local, send_1, recv_1, send_2, recv_2, send_3, recv_3 = sems

    def place(device, k):
        return out.at[pl.ds(k * ROWS, ROWS), pl.ds(pl.multiple_of(device * own, own), own)]

    def remote(src, dst, send, recv, device):
        return pltpu.make_async_remote_copy(
            src_ref=src, dst_ref=dst, send_sem=send, recv_sem=recv, device_id={"tensor": device}, device_id_type=MESH
        )

    def chunk(k):
        return act.at[pl.ds(k * ROWS, ROWS)]

    near = [remote(chunk(k), place(along, k), send_1.at[k], recv_1.at[k], mate) for k in range(CHUNKS)]
    over = [remote(chunk(k), place(along, k), send_2.at[k], recv_2.at[k], far) for k in range(CHUNKS)]
    pass_on = [remote(place(far, k), place(far, k), send_3.at[k], recv_3.at[k], mate) for k in range(CHUNKS)]
    kept = [pltpu.make_async_copy(chunk(k), place(along, k), local.at[k]) for k in range(CHUNKS)]

    def launch(k):
        over[k].start()
        near[k].start()
        kept[k].start()

    for k in range(CHUNKS):
        fill(k)
        if k:
            launch(k - 1)
    launch(CHUNKS - 1)
    for k in range(CHUNKS):
        over[k].wait_recv()
        pass_on[k].start()
    for k in range(CHUNKS):
        near[k].wait()
        over[k].wait_send()
        pass_on[k].wait()
        kept[k].wait()


SCATTER_SEMS = [pltpu.SemaphoreType.DMA((2,))] + [pltpu.SemaphoreType.DMA((2, CHUNKS))] * 2 + [pltpu.SemaphoreType.DMA((CHUNKS,))] * 2
GATHER_SEMS = [pltpu.SemaphoreType.DMA((CHUNKS,))] * 7


def forward_kernel(dp, tensor, own, scatter, gather, x, counts, mask, gain, bias, xhat, rstd, act, *scratch):
    group = Group(dp, tensor, True)
    along = lax.axis_index("tensor")
    scratch = list(scratch)
    note, box, sems = scratch[:3]
    scratch = scratch[3:]
    barrier = group.greet()
    h = x
    if scatter:
        h, pair, cross, arrived = scratch[:4]
        group.meet(barrier)
        scatter_frames(x, h, pair, cross, arrived, scratch[4:9], along, own)
        scratch = scratch[9:]
    keep = mask[...]
    zero = jnp.zeros(keep.shape, jnp.float32)
    mine = counts[group.me]
    mean = jnp.sum(positions(lambda i, acc: acc + h[i], zero) * keep, axis=0, keepdims=True) / jnp.maximum(mine, 1.0)

    def square(i, acc):
        off = h[i] - mean
        return acc + off * off

    second = jnp.sum(positions(square, zero) * keep, axis=0, keepdims=True)
    to_tile(note, mean, second)
    if not scatter:
        group.meet(barrier)
    group.exchange(note, box, sems)
    mean, scale = combine_moments(box, counts, group.size)
    mean, scale = to_row(mean), to_row(scale)
    rstd[...] = scale
    gains, biases = gain[...], bias[...]
    spread = scratch[0] if gather else act

    def finish(i, carry):
        normed = (h[i] - mean) * scale
        xhat[i] = normed
        spread[i] = jnp.maximum(gains * normed + biases, 0.0)
        return carry

    if gather:
        fill = lambda k: lax.fori_loop(k * ROWS, (k + 1) * ROWS, finish, 0)
        gather_frames(fill, spread, act, scratch[1:8], along, own)
    else:
        positions(finish, 0)


def backward_kernel(dp, tensor, own, scatter, gather, x, counts, mask, gain, bias, rstd, xhat, sums, back, *scratch):
    group = Group(dp, tensor, True)
    along = lax.axis_index("tensor")
    scratch = list(scratch)
    note, box, sems = scratch[:3]
    scratch = scratch[3:]
    barrier = group.greet()
    d = x
    if scatter:
        d, pair, cross, arrived = scratch[:4]
        group.meet(barrier)
        scatter_frames(x, d, pair, cross, arrived, scratch[4:9], along, own)
        scratch = scratch[9:]
    gains, biases = gain[...], bias[...]
    zero = jnp.zeros(mask.shape, jnp.float32)

    def through(i):
        return jnp.where(gains * xhat[i] + biases > 0, d[i], 0.0)

    def add(i, acc):
        grad = through(i)
        return acc[0] + grad, acc[1] + grad * xhat[i]

    first, second = positions(add, (zero, zero))
    to_tile(note, jnp.sum(first, axis=0, keepdims=True), jnp.sum(second, axis=0, keepdims=True))
    if not scatter:
        group.meet(barrier)
    group.exchange(note, box, sems)
    total = lax.fori_loop(0, group.size, lambda i, acc: acc + box[i], jnp.zeros((8, 128), jnp.float32))
    sums[...] = total
    shared = total / counts[group.size]
    first, second = to_row(shared[0:4]), to_row(shared[4:8])
    factor = gains * rstd[...]
    keep = mask[...]
    spread = scratch[0] if gather else back

    def finish(i, carry):
        spread[i] = factor * (through(i) - keep * (first + xhat[i] * second))
        return carry

    if gather:
        fill = lambda k: lax.fori_loop(k * ROWS, (k + 1) * ROWS, finish, 0)
        gather_frames(fill, spread, back, scratch[1:8], along, own)
    else:
        positions(finish, 0)


def narrow_norm(number, mode, sizes, x, *operands, scatter=False, gather=False):
    dp, tensor, frames, chans = sizes
    own = frames // tensor
    block = (CELLS, own, chans)
    flat = dp * tensor
    scratch = [pltpu.VMEM((8, 128), jnp.float32), pltpu.VMEM((flat, 8, 128), jnp.float32), pltpu.SemaphoreType.DMA((2,))]
    if scatter:
        scratch += [pltpu.VMEM(block, jnp.float32), pltpu.VMEM((2,) + block, jnp.float32)]
        scratch += [pltpu.VMEM(block, jnp.float32)] * 2 + SCATTER_SEMS
    if gather:
        scratch += [pltpu.VMEM(block, jnp.float32)] + GATHER_SEMS
    last = shape(CELLS, frames, chans) if gather else shape(*block)
    if mode == "forward":
        kernel, outs = forward_kernel, (shape(*block), shape(1, chans), last)
    else:
        kernel, outs = backward_kernel, (shape(8, 128), last)
    return pl.pallas_call(
        functools.partial(kernel, dp, tensor, own, scatter, gather),
        out_shape=outs,
        in_specs=[HBM if scatter else VMEM, SMEM] + [VMEM] * (len(operands) - 1),
        out_specs=tuple([VMEM] * (len(outs) - 1) + [HBM if gather else VMEM]),
        scratch_shapes=scratch,
        compiler_params=params(number, 24),
        name="narrow_" + mode,
    )(x, *operands)


def wide_kernel(dp, tensor, moments_mode, x, counts, out, box, sems):
    group = Group(dp, tensor, False)
    group.meet(group.greet())
    group.exchange(x, box, sems)
    if moments_mode:
        mean, scale = combine_moments(box, counts, group.size)
        out[0:4] = mean
        out[4:8] = scale
    else:
        out[...] = lax.fori_loop(0, group.size, lambda i, acc: acc + box[i], jnp.zeros((8, 128), jnp.float32))


def wide_exchange(number, sizes, counts, first, second, moments_mode):
    dp, tensor = sizes[:2]
    tile = jnp.concatenate([first.reshape(4, 128), second.reshape(4, 128)])
    out = pl.pallas_call(
        functools.partial(wide_kernel, dp, tensor, moments_mode),
        out_shape=shape(8, 128),
        in_specs=[VMEM, SMEM],
        out_specs=VMEM,
        scratch_shapes=[pltpu.VMEM((dp, 8, 128), jnp.float32), pltpu.SemaphoreType.DMA((2,))],
        compiler_params=params(number, 4),
        name="wide_exchange",
    )(tile, counts)
    return out[0:4].reshape(-1), out[4:8].reshape(-1)


def wide_moments(number, sizes, counts, h, mask, here):
    mean = jnp.sum(h * mask, axis=(0, 1)) / jnp.maximum(here, 1.0)
    second = jnp.sum(mask * (h - mean) ** 2, axis=(0, 1))
    return wide_exchange(number, sizes, counts, mean, second, True)


def wide_back(number, sizes, counts, grad, xhat, mask, gain, rstd):
    first, second = jnp.sum(grad, axis=(0, 1)), jnp.sum(grad * xhat, axis=(0, 1))
    first, second = wide_exchange(number, sizes, counts, first, second, False)
    return gain * rstd * (grad - mask * (first + xhat * second) / counts[sizes[0]]), second, first


def shift_from(value, steps):
    count = lax.axis_size("tensor")
    initial, last = (max(0, -steps), min(count, count - steps))
    return lax.ppermute(value, "tensor", [(s, s + steps) for s in range(initial, last)])


def halo(x, width):
    left = shift_from(x[:, x.shape[1] - width :], 1)
    right = shift_from(x[:, :width], -1)
    return jnp.concatenate([left, x, right], axis=1)


def later(x):
    return jnp.concatenate([x[:, 1:], jnp.zeros_like(x[:, :1])], axis=1)


def earlier(x):
    return jnp.concatenate([jnp.zeros_like(x[:, :1]), x[:, :-1]], axis=1)


def local(
    features, frame_clip, reduce_first, gain_reduce, bias_reduce, motion_down, motion_kernel, motion_up,
    motion_bias, group_taps, group_spatial, gain_groups, bias_groups, expand_first, gain_expand, bias_expand,
    reduce_second, gain_narrow, bias_narrow, spatial_second, gain_spatial, bias_spatial, expand_second,
    gain_output, bias_output, cotangent,
):
    tensor = lax.axis_size("tensor")
    at = lax.axis_index("tensor")
    frames = features.shape[0]
    own = frames // tensor
    gw = group_taps.shape[2]
    rank = motion_down.shape[1]
    groups = tensor
    reach = groups
    x = jnp.transpose(features, (1, 0, 2))
    seed = jnp.transpose(cotangent, (1, 0, 2))

    valid = (frame_clip >= 0).astype(jnp.float32)
    sizes = (lax.axis_size("dp"), tensor, frames, tensor * group_taps.shape[2])
    parts = lax.all_gather(jnp.sum(valid.reshape(tensor, own), axis=1) * CELLS, "dp")
    count = jnp.sum(parts)
    counts = jnp.concatenate([parts.reshape(-1), count[None]])
    wide_counts = jnp.concatenate([jnp.sum(parts, axis=1), count[None]])
    here_count = jnp.sum(valid) * CELLS
    wide_mask = valid[None, :, None]
    padded = jnp.pad(frame_clip, (reach + 1, reach + 1), constant_values=-2)
    clips = lax.dynamic_slice(padded, (at * own,), (own + 2 * reach + 2,))
    here = clips[1:-1]
    next_ext = ((here >= 0) & (clips[2:] == here)).astype(jnp.float32)[None, :, None]
    prev_ext = ((here >= 0) & (clips[:-2] == here)).astype(jnp.float32)[None, :, None]
    mask = (here >= 0).astype(jnp.float32)[reach : reach + own][None, :, None]
    next_own = next_ext[0, reach : reach + own]
    mask = jnp.broadcast_to(mask[0], (own, sizes[3]))

    rows = lambda w: lax.all_to_all(w, "tensor", 0, 1, tiled=True)
    cols = lambda w: lax.all_to_all(w, "tensor", 1, 0, tiled=True)
    w_reduce, w_reduce2 = rows(reduce_first), rows(reduce_second)
    w_expand, w_expand2 = cols(expand_first), cols(expand_second)
    small = jnp.concatenate(
        [
            motion_down.T, motion_up, motion_bias[None], gain_reduce[None], bias_reduce[None], gain_groups[None],
            bias_groups[None], gain_narrow[None], bias_narrow[None], gain_spatial[None], bias_spatial[None],
            group_taps[0],
        ],
        axis=0,
    )
    small = lax.all_gather(small, "tensor", axis=1, tiled=True)
    md, mu = small[:rank].T, small[rank : 2 * rank]
    mb, g_red, b_red, g_grp, b_grp, g_nar, b_nar, g_spa, b_spa = [small[2 * rank + i : 2 * rank + i + 1] for i in range(9)]
    taps = small[2 * rank + 9 : 2 * rank + 12]
    spatial = lax.all_gather(spatial_second, "tensor", axis=1, tiled=True)
    group_w = lax.all_gather(group_spatial, "tensor", axis=0, tiled=True)

    p1 = mm(x, w_reduce, FWD)
    xh1, r1, act1 = narrow_norm(0, "forward", sizes, p1, counts, mask, g_red, b_red, scatter=True)

    edges = jnp.asarray(edge_mask())
    w_pos = jnp.sum(edges[:, :, None] * motion_kernel[None], axis=1)
    motion = mm(act1, md, FWD)
    ahead = jnp.sum(motion * w_pos[:, None, :], axis=0)
    base = jnp.sum(motion, axis=0)
    follow = jnp.concatenate([ahead[1:], shift_from(ahead[:1], -1)], axis=0)
    pooled = next_own * (follow - base) / CELLS
    gate = jax.nn.sigmoid(jnp.dot(pooled, mu, precision=FWD) + mb)
    excited = act1 * gate[None]
    exc = halo(excited, reach)
    ins, mids, outs = [], [], []
    carry = 0.0
    mine = slice(reach, reach + own)
    for g in range(groups):
        part = slice(g * gw, (g + 1) * gw)
        u = exc[:, :, part] + carry
        k = taps[:, part]
        stacked = stack9(k[0] * earlier(u) * prev_ext + k[1] * u + k[2] * later(u) * next_ext)
        carry = mm(stacked, group_w[g], FWD)
        ins.append(u)
        mids.append(stacked[:, mine])
        outs.append(carry[:, mine])
    grouped = jnp.concatenate(outs, axis=-1)
    xh2, r2, mixed = narrow_norm(1, "forward", sizes, grouped, counts, mask, g_grp, b_grp, gather=True)
    h3 = mm(mixed, w_expand, FWD)
    mean3, r3 = wide_moments(2, sizes, wide_counts, h3, wide_mask, here_count)
    xh3 = (h3 - mean3) * r3
    pre3 = gain_expand * xh3 + bias_expand + x
    middle = jnp.maximum(pre3, 0.0)

    p4 = mm(middle, w_reduce2, FWD)
    xh4, r4, act4 = narrow_norm(3, "forward", sizes, p4, counts, mask, g_nar, b_nar, scatter=True)
    stacked4 = stack9(act4)
    h5 = mm(stacked4, spatial, FWD)
    xh5, r5, conv_act = narrow_norm(4, "forward", sizes, h5, counts, mask, g_spa, b_spa, gather=True)
    h6 = mm(conv_act, w_expand2, FWD)
    mean6, r6 = wide_moments(5, sizes, wide_counts, h6, wide_mask, here_count)
    xh6 = (h6 - mean6) * r6
    pre6 = gain_output * xh6 + bias_output + middle
    output = wide_mask * jnp.maximum(pre6, 0.0)

    d_last = jnp.where(pre6 > 0, seed * wide_mask, 0.0)
    d6, gg_output, gb_output = wide_back(6, sizes, wide_counts, d_last, xh6, wide_mask, gain_output, r6)
    gw_expand2 = outer(conv_act, d6, GRAD)
    s5, d5 = narrow_norm(7, "backward", sizes, mm_t(d6, w_expand2, BWD), counts, mask, g_spa, b_spa, r5, xh5, scatter=True)
    gw_spatial = outer(stacked4, d5, GRAD)
    d_act4 = mm(stack9(d5), flip_taps(spatial, d5.shape[2]), BWD)
    s4, d4_all = narrow_norm(8, "backward", sizes, d_act4, counts, mask, g_nar, b_nar, r4, xh4, gather=True)
    gw_reduce2 = outer(middle, d4_all, GRAD)
    d_pre3 = jnp.where(pre3 > 0, d_last + mm_t(d4_all, w_reduce2, BWD), 0.0)

    d3, gg_expand, gb_expand = wide_back(9, sizes, wide_counts, d_pre3, xh3, wide_mask, gain_expand, r3)
    gw_expand = outer(mixed, d3, GRAD)
    s2, d2 = narrow_norm(10, "backward", sizes, mm_t(d3, w_expand, BWD), counts, mask, g_grp, b_grp, r2, xh2, scatter=True)
    d2_ext = halo(d2, reach)
    d_exc, gw_group, g_taps = [None] * groups, [None] * groups, [None] * groups
    carry = 0.0
    for g in reversed(range(groups)):
        part = slice(g * gw, (g + 1) * gw)
        k = taps[:, part]
        dy = d2_ext[:, :, part] + carry
        gw_group[g] = outer(mids[g], dy[:, mine], GRAD)
        dt = mm(stack9(dy), flip_taps(group_w[g], gw), BWD)
        u = ins[g]
        g_taps[g] = jnp.stack(
            [
                jnp.sum((dt * prev_ext * earlier(u))[:, mine], axis=(0, 1)),
                jnp.sum((dt * u)[:, mine], axis=(0, 1)),
                jnp.sum((dt * next_ext * later(u))[:, mine], axis=(0, 1)),
            ]
        )
        carry = k[0] * later(dt * prev_ext) + k[1] * dt + k[2] * earlier(dt * next_ext)
        d_exc[g] = carry[:, mine]
    d_exc = jnp.concatenate(d_exc, axis=-1)
    d_gate = jnp.sum(d_exc * act1, axis=0) * gate * (1.0 - gate)
    g_mb = jnp.sum(d_gate, axis=0)
    g_mu = lax.dot_general(pooled, d_gate, (((0,), (0,)), ((), ())), precision=FWD)
    d_pool = mm_t(d_gate, mu, FWD) * next_own / CELLS
    d_ahead = jnp.concatenate([shift_from(d_pool[-1:], 1), d_pool[:-1]], axis=0)
    g_pos = jnp.sum(motion * d_ahead[None], axis=1)
    g_mk = jnp.sum(edges[:, :, None] * g_pos[:, None, :], axis=0)
    d_motion = w_pos[:, None, :] * d_ahead[None] - d_pool[None]
    g_md = outer(act1, d_motion, FWD)
    d_act1 = d_exc * gate[None] + mm_t(d_motion, md, FWD)
    s1, d1_all = narrow_norm(11, "backward", sizes, d_act1, counts, mask, g_red, b_red, r1, xh1, gather=True)
    gw_reduce = outer(x, d1_all, GRAD)
    grad_features = d_pre3 + mm_t(d1_all, w_reduce, BWD)

    gw_spatial = lax.psum_scatter(gw_spatial, "tensor", scatter_dimension=1, tiled=True)
    gw_group = lax.psum_scatter(jnp.stack(gw_group), "tensor", scatter_dimension=0, tiled=True)
    big = lax.psum(
        (cols(gw_reduce), rows(gw_expand), cols(gw_reduce2), rows(gw_expand2), gw_spatial, gw_group), "dp"
    )
    tiny = jnp.concatenate([g_md.T, g_mu, g_mb[None], jnp.concatenate(g_taps, axis=-1)], axis=0)
    tiny, g_mk = lax.psum((tiny, g_mk), BOTH)
    pairs = [total.reshape(2, -1)[::-1] for total in (s1, s2, s4, s5)]
    narrow = jnp.concatenate(pairs)
    tiny = lax.dynamic_slice(jnp.concatenate([tiny, narrow]), (0, at * gw), (2 * rank + 12, gw))
    vec = tiny[2 * rank + 4 :]
    return (
        jnp.transpose(output, (1, 0, 2)),
        jnp.transpose(grad_features, (1, 0, 2)),
        big[0],
        vec[0],
        vec[1],
        tiny[:rank].T,
        g_mk,
        tiny[rank : 2 * rank],
        tiny[2 * rank],
        tiny[2 * rank + 1 : 2 * rank + 4][None],
        big[5],
        vec[2],
        vec[3],
        big[1],
        gg_expand,
        gb_expand,
        big[2],
        vec[4],
        vec[5],
        big[4],
        vec[6],
        vec[7],
        big[3],
        gg_output,
        gb_output,
    )


def solution(mesh):
    wide, col, row, chan, deep = P("dp", None, "tensor"), P(None, "tensor"), P("tensor", None), P("tensor"), P("tensor", None, None)
    return jax.shard_map(
        local,
        mesh=mesh,
        in_specs=(wide, P("dp"), col, chan, chan, row, P(), col, chan, deep, deep, chan, chan, row, chan, chan, col, chan, chan, col, chan, chan, row, chan, chan, wide),
        out_specs=(wide, wide, col, chan, chan, row, P(), col, chan, deep, deep, chan, chan, row, chan, chan, col, chan, chan, col, chan, chan, row, chan, chan),
        check_vma=False,
    )
```
